32 devices in a mesh: dp: 4 (over z), row: 4 (over x, core), col: 2 (over y).
Axes of the slice: x: 2, y: 2, z: 4, core: 2. Of those that a mesh axis runs over, the one named last changes fastest.
Arguments:
- block_input: float32 [23328, 1152], P(('dp', 'row'), 'col'), may hold values from -32 to 32
- qkv_weight: bfloat16 [3, 1152, 1152], P(None, 'col', 'row'), may hold values from -0.1875 to 0.1875
- query_bias: float32 [1152], P('row'), may hold values from -3 to 3
- value_bias: float32 [1152], P('row'), may hold values from -3 to 3
- out_weight: bfloat16 [1152, 1152], P('row', 'col'), may hold values from -0.75 to 0.75
- out_bias: float32 [1152], P('col'), may hold values from -2 to 2
- first_gain: float32 [1152], P('col'), may hold values from 0.3 to 2.4
- first_shift: float32 [1152], P('col'), may hold values from -2 to 2
- second_gain: float32 [1152], P('col'), may hold values from 0.3 to 2.4
- second_shift: float32 [1152], P('col'), may hold values from -2 to 2
- up_weight: bfloat16 [1152, 4304], P('col', 'row'), may hold values from -0.1875 to 0.1875
- up_bias: float32 [4304], P('row'), may hold values from -3 to 3
- down_weight: bfloat16 [4304, 1152], P('row', 'col'), may hold values from -0.09375 to 0.09375
- down_bias: float32 [1152], P('col'), may hold values from -3 to 3
- out_cotangent: float32 [23328, 1152], P(('dp', 'row'), 'col'), may hold values from -6 to 6
Outputs:
- block_output: float32 [23328, 1152], P(('dp', 'row'), 'col')
- input_grad: float32 [23328, 1152], P(('dp', 'row'), 'col')
- qkv_grad: float32 [3, 1152, 1152], P(None, 'col', 'row')
- query_bias_grad: float32 [1152], P('row')
- value_bias_grad: float32 [1152], P('row')
- out_weight_grad: float32 [1152, 1152], P('row', 'col')
- out_bias_grad: float32 [1152], P('col')
- first_gain_grad: float32 [1152], P('col')
- first_shift_grad: float32 [1152], P('col')
- second_gain_grad: float32 [1152], P('col')
- second_shift_grad: float32 [1152], P('col')
- up_weight_grad: float32 [1152, 4304], P('col', 'row')
- up_bias_grad: float32 [4304], P('row')
- down_weight_grad: float32 [4304, 1152], P('row', 'col')
- down_bias_grad: float32 [1152], P('col')
The draws below stay inside these ranges and needn't reach their ends.
All inputs are finite; a program needn't handle non-finite values.
Results may differ from the reference program's by a relative error of at most 0.03.
Values may be sent and summed in bfloat16 or wider, within the bound.
No kernel may reach another device: no remote copies, remote signals or barrier semaphores. Data moves between devices by JAX's collectives and lax.ppermute only.
A program may use at most 320 MiB of HBM per device.

```python
import jax
import jax.numpy as jnp
from jax import lax

D = 1152
H = 16
HD = 72
F = 4304
S = 729
IMAGES = 32
TOKENS = 23328
N_ROW = 4
N_COL = 2


def draw_block_input(key, part):
    key_base, key_column, key_row = jax.random.split(key, 3)
    column = jnp.arange(D, dtype=jnp.float32) / D
    base = jnp.clip(jax.random.normal(key_base, (TOKENS, D), jnp.float32), -4.0, 4.0)
    column_scale = 0.3 * jnp.power(10.0, column)[None, :] * jax.random.uniform(key_column, (1, D), jnp.float32, 0.7, 1.3)
    row_scale = jnp.exp(jax.random.uniform(key_row, (TOKENS, 1), jnp.float32, -0.6931, 0.6931))
    return base * column_scale * row_scale


def gain_ramp(key, salt, low, high, spread):
    noise_key = jax.random.fold_in(key, salt)
    position = jnp.arange(D, dtype=jnp.float32) / max(D - 1, 1)
    ramp = low * jnp.power(high / low, position)
    noise = jax.random.uniform(noise_key, (D,), jnp.float32, 1.0 - spread, 1.0 + spread)
    return ramp * noise


def draw_first_gain(key, part):
    return gain_ramp(key, 11, 0.5, 1.5, 0.2)


def draw_second_gain(key, part):
    return gain_ramp(key, 23, 0.5, 1.5, 0.2)


def level_of(stream_key, shape, cuts, least, top_value):
    def one(dim, parts):
        steps = jax.random.uniform(jax.random.fold_in(jax.random.fold_in(stream_key, 6), dim), (parts,), jnp.float32, least / len(cuts), top_value / len(cuts))
        return jnp.repeat(jnp.exp(steps), shape[dim] // parts).reshape((-1,) + (1,) * (len(shape) - dim - 1))

    factor_of = one(*cuts[0])
    for cut in cuts[1:]:
        factor_of = factor_of * one(*cut)
    return factor_of


def gaussian(key, dims, scale, most, cuts=(), held_as=jnp.bfloat16):
    drawn = jax.random.normal(key, dims, jnp.float32) * scale
    if len(cuts) > 0:
        drawn = level_of(key, dims, cuts, -0.22, 0.18) * drawn
    return jnp.clip(drawn, min=-most, max=most).astype(held_as)


def setup_inputs(seed: int = 0) -> dict:
    streams_of = jax.random.split(jax.random.key(seed), 16)
    block_input = draw_block_input(jax.random.fold_in(streams_of[15], 71), 0)
    qkv_weight = gaussian(streams_of[1], (3, D, D), D ** -0.5, 0.1875, ((1, 2), (2, 4)))
    query_bias = gaussian(streams_of[2], (D,), 0.5, 3.0, ((0, 4),), jnp.float32)
    value_bias = gaussian(streams_of[3], (D,), 0.5, 3.0, ((0, 4),), jnp.float32)
    out_weight = gaussian(streams_of[4], (D, D), (max(4, D // 16)) ** -0.5, 0.75, ((0, 4), (1, 2)))
    out_bias = gaussian(streams_of[5], (D,), 0.3, 2.0, ((0, 2),), jnp.float32)
    first_gain = draw_first_gain(jax.random.fold_in(streams_of[15], 71), 0)
    first_shift = gaussian(streams_of[7], (D,), 0.3, 2.0, ((0, 2),), jnp.float32)
    second_gain = draw_second_gain(jax.random.fold_in(streams_of[15], 71), 0)
    second_shift = gaussian(streams_of[9], (D,), 0.3, 2.0, ((0, 2),), jnp.float32)
    up_weight = gaussian(streams_of[10], (D, F), D ** -0.5, 0.1875, ((0, 2), (1, 4)))
    up_bias = gaussian(streams_of[11], (F,), 0.5, 3.0, ((0, 4),), jnp.float32)
    down_weight = gaussian(streams_of[12], (F, D), F ** -0.5, 0.09375, ((0, 4), (1, 2)))
    down_bias = gaussian(streams_of[13], (D,), 0.6, 3.0, ((0, 2),), jnp.float32)
    out_cotangent = gaussian(streams_of[14], (TOKENS, D), 1.0, 6.0, ((0, 16), (1, 2)), jnp.float32)
    return {"block_input": block_input, "qkv_weight": qkv_weight, "query_bias": query_bias, "value_bias": value_bias, "out_weight": out_weight, "out_bias": out_bias, "first_gain": first_gain, "first_shift": first_shift, "second_gain": second_gain, "second_shift": second_shift, "up_weight": up_weight, "up_bias": up_bias, "down_weight": down_weight, "down_bias": down_bias, "out_cotangent": out_cotangent}


EPSILON = 1e-06

def rounded(tensor):
    return lax.optimization_barrier(tensor.astype(jnp.bfloat16)).astype(jnp.float32)

def split_dot(left, right, pieces):
    row_count = left.shape[0]
    inner_len = left.shape[1] // pieces
    left_blocks = left.astype(jnp.float32).reshape(row_count, pieces, inner_len)
    right_blocks = right.astype(jnp.float32).reshape(pieces, inner_len, right.shape[1])
    partials = jnp.einsum('tpk,pkn->ptn', left_blocks, right_blocks)
    return lax.optimization_barrier(jnp.sum(rounded(partials), axis=0))

def gelu_tanh(tensor):
    return jax.nn.gelu(tensor, approximate=True)

def norm_forward(values, norm_gain, norm_shift):
    mean_val = lax.optimization_barrier(jnp.mean(values, axis=-1, keepdims=True))
    mean_square = lax.optimization_barrier(jnp.mean(values * values, axis=-1, keepdims=True))
    var_val = mean_square - mean_val * mean_val
    centered = values - mean_val
    inv_dev = lax.rsqrt(var_val + EPSILON)
    normed = centered * inv_dev
    return ((normed * norm_gain + norm_shift).astype(jnp.bfloat16), normed, inv_dev)

def norm_backward(grad_out, normed, inv_dev, norm_gain):
    scaled = grad_out * norm_gain
    first_mean = lax.optimization_barrier(jnp.mean(scaled, axis=-1, keepdims=True))
    second_mean = lax.optimization_barrier(jnp.mean(scaled * normed, axis=-1, keepdims=True))
    return inv_dev * (scaled - first_mean - normed * second_mean)

def attend(query_rows, key_rows, value_rows):
    score_scale = HD ** (-0.5)
    scores = jnp.einsum('shd,thd->hst', query_rows.astype(jnp.float32), key_rows.astype(jnp.float32)) * score_scale
    row_top = lax.optimization_barrier(jnp.max(scores, axis=-1, keepdims=True))
    logsum = row_top + jnp.log(lax.optimization_barrier(jnp.sum(jnp.exp(scores - row_top), axis=-1, keepdims=True)))
    soft_weights = rounded(jnp.exp(scores - logsum))
    attended = jnp.einsum('hst,thd->shd', soft_weights, value_rows.astype(jnp.float32)).astype(jnp.bfloat16)
    return (attended, logsum)

def attend_back(query_rows, key_rows, value_rows, logsum, grad_attended):
    score_scale = HD ** (-0.5)
    query_f32 = query_rows.astype(jnp.float32)
    key_f32 = key_rows.astype(jnp.float32)
    value_f32 = value_rows.astype(jnp.float32)
    grad_f32 = grad_attended.astype(jnp.float32)
    scores = jnp.einsum('shd,thd->hst', query_f32, key_f32) * score_scale
    soft = jnp.exp(scores - logsum)
    grad_value = jnp.einsum('hst,shd->thd', rounded(soft), grad_f32)
    grad_soft = jnp.einsum('shd,thd->hst', grad_f32, value_f32)
    row_delta = lax.optimization_barrier(jnp.sum(soft * grad_soft, axis=-1, keepdims=True))
    grad_scores = rounded(soft * (grad_soft - row_delta))
    grad_query = jnp.einsum('hst,thd->shd', grad_scores, key_f32) * score_scale
    grad_key = jnp.einsum('hst,shd->thd', grad_scores, query_f32) * score_scale
    return (grad_query.astype(jnp.bfloat16), grad_key.astype(jnp.bfloat16), grad_value.astype(jnp.bfloat16))

def reference(block_input, qkv_weight, query_bias, value_bias, out_weight, out_bias, first_gain, first_shift, second_gain, second_shift, up_weight, up_bias, down_weight, down_bias, out_cotangent):
    inputs_img = block_input.reshape(IMAGES, S, D)
    cot_img = out_cotangent.reshape(IMAGES, S, D)
    zero_grads = (jnp.zeros((3, D, D), jnp.float32), jnp.zeros((D,), jnp.float32), jnp.zeros((D,), jnp.float32), jnp.zeros((D, D), jnp.float32), jnp.zeros((D,), jnp.float32), jnp.zeros((D,), jnp.float32), jnp.zeros((D,), jnp.float32), jnp.zeros((D,), jnp.float32), jnp.zeros((D,), jnp.float32), jnp.zeros((D, F), jnp.float32), jnp.zeros((F,), jnp.float32), jnp.zeros((F, D), jnp.float32), jnp.zeros((D,), jnp.float32))

    def image_step(totals, pair):
        image_in, image_cot = pair
        first_normed, first_hat, first_inv = norm_forward(image_in, first_gain, first_shift)
        proj_query = split_dot(first_normed, qkv_weight[0], N_COL)
        proj_key = split_dot(first_normed, qkv_weight[1], N_COL)
        proj_value = split_dot(first_normed, qkv_weight[2], N_COL)
        query_rows = (proj_query + query_bias).astype(jnp.bfloat16).reshape(S, H, HD)
        key_rows = proj_key.astype(jnp.bfloat16).reshape(S, H, HD)
        value_rows = (proj_value + value_bias).astype(jnp.bfloat16).reshape(S, H, HD)
        attended, logsum = attend(query_rows, key_rows, value_rows)
        attended_flat = attended.reshape(S, D)
        middle = image_in + split_dot(attended_flat, out_weight, N_ROW) + out_bias
        second_normed, second_hat, second_inv = norm_forward(middle, second_gain, second_shift)
        pre_act = split_dot(second_normed, up_weight, N_COL) + up_bias
        hidden = gelu_tanh(pre_act).astype(jnp.bfloat16)
        block_out = middle + split_dot(hidden, down_weight, N_ROW) + down_bias
        cot_rounded = image_cot.astype(jnp.bfloat16)
        down_w_grad = jnp.dot(hidden.T, cot_rounded, preferred_element_type=jnp.float32)
        down_b_grad = lax.optimization_barrier(jnp.sum(cot_rounded.astype(jnp.float32), axis=0))
        grad_hidden = split_dot(cot_rounded, down_weight.T, N_COL)
        grad_pre = jax.vjp(gelu_tanh, pre_act)[1](grad_hidden)[0].astype(jnp.bfloat16)
        up_w_grad = jnp.dot(second_normed.T, grad_pre, preferred_element_type=jnp.float32)
        up_b_grad = lax.optimization_barrier(jnp.sum(grad_pre.astype(jnp.float32), axis=0))
        grad_second = split_dot(grad_pre, up_weight.T, N_ROW)
        second_gain_part = lax.optimization_barrier(jnp.sum(grad_second * second_hat, axis=0))
        second_shift_part = lax.optimization_barrier(jnp.sum(grad_second, axis=0))
        grad_middle = image_cot + norm_backward(grad_second, second_hat, second_inv, second_gain)
        middle_rounded = grad_middle.astype(jnp.bfloat16)
        out_w_grad = jnp.dot(attended_flat.T, middle_rounded, preferred_element_type=jnp.float32)
        out_b_grad = lax.optimization_barrier(jnp.sum(middle_rounded.astype(jnp.float32), axis=0))
        grad_attended = split_dot(middle_rounded, out_weight.T, N_COL).astype(jnp.bfloat16).reshape(S, H, HD)
        grad_query, grad_key, grad_value = attend_back(query_rows, key_rows, value_rows, logsum, grad_attended)
        query_flat = grad_query.reshape(S, D)
        key_flat = grad_key.reshape(S, D)
        value_flat = grad_value.reshape(S, D)
        qkv_w_grad = jnp.stack([jnp.dot(first_normed.T, query_flat, preferred_element_type=jnp.float32), jnp.dot(first_normed.T, key_flat, preferred_element_type=jnp.float32), jnp.dot(first_normed.T, value_flat, preferred_element_type=jnp.float32)])
        query_b_grad = lax.optimization_barrier(jnp.sum(query_flat.astype(jnp.float32), axis=0))
        value_b_grad = lax.optimization_barrier(jnp.sum(value_flat.astype(jnp.float32), axis=0))
        stacked = jnp.stack([query_flat, key_flat, value_flat]).astype(jnp.float32).reshape(3, S, N_ROW, D // N_ROW)
        weight_blocks = qkv_weight.astype(jnp.float32).reshape(3, D, N_ROW, D // N_ROW)
        grad_first = lax.optimization_barrier(jnp.sum(rounded(jnp.einsum('jsrk,jdrk->rsd', stacked, weight_blocks)), axis=0))
        first_gain_part = lax.optimization_barrier(jnp.sum(grad_first * first_hat, axis=0))
        first_shift_part = lax.optimization_barrier(jnp.sum(grad_first, axis=0))
        grad_in = grad_middle + norm_backward(grad_first, first_hat, first_inv, first_gain)
        extras = (qkv_w_grad, query_b_grad, value_b_grad, out_w_grad, out_b_grad, first_gain_part, first_shift_part, second_gain_part, second_shift_part, up_w_grad, up_b_grad, down_w_grad, down_b_grad)
        new_totals = tuple((total + extra for total, extra in zip(totals, extras)))
        return (new_totals, (block_out, grad_in))
    totals, (outputs, input_grads) = lax.scan(image_step, zero_grads, (inputs_img, cot_img))
    grads = [total / IMAGES for total in totals]
    return (outputs.reshape(TOKENS, D), input_grads.reshape(TOKENS, D), grads[0], grads[1], grads[2], grads[3], grads[4], grads[5], grads[6], grads[7], grads[8], grads[9], grads[10], grads[11], grads[12])
```

```python
import jax
import jax.numpy as jnp
from jax import lax
from jax.sharding import PartitionSpec as P

HD = 72
S = 729
EPSILON = 1e-06
BF = jnp.bfloat16
F32 = jnp.float32


def gelu_tanh(tensor):
    return jax.nn.gelu(tensor, approximate=True)


def swap(array, axis, mask):
    size = lax.axis_size(axis)
    return lax.ppermute(array, axis, [(i, i ^ mask) for i in range(size)])


def over_x(array):
    return swap(array, "row", 2)


def over_core(array):
    return swap(array, "row", 1)


def over_y(array):
    return swap(array, "col", 1)


def dot(left, right, dims):
    return lax.dot_general(left, right, (dims, ((), ())), preferred_element_type=F32)


def halves(array):
    half = array.shape[0] // 2
    return [array[:half], array[half:]]


def gather_weight(shard):
    own = halves(shard)
    far_x = [over_x(part) for part in own]
    far_y = [over_y(part) for part in own]
    diagonal = [over_y(far_x[0]), over_x(far_y[1])]
    pieces = {(0, 0): own, (2, 0): far_x, (0, 1): far_y, (2, 1): diagonal}
    for (k, m), parts in list(pieces.items()):
        pieces[k ^ 1, m] = [over_core(part) for part in parts]
    return pieces


def stack_pieces(pieces):
    return [
        jnp.concatenate(pieces[k, 0] + pieces[k, 1], axis=0) for k in range(4)
    ]


def scatter_grad(grads):
    chip = {}
    for k in (0, 2):
        for m in (0, 1):
            came = over_core(grads[k ^ 1, m].astype(BF))
            chip[k, m] = halves((grads[k, m] + came.astype(F32)).astype(BF))

    def plus(one, two):
        return (one.astype(F32) + two.astype(F32)).astype(BF)

    diagonal = chip[2, 1]
    to_y = [plus(chip[0, 1][0], over_x(diagonal[0])), chip[0, 1][1]]
    to_x = [chip[2, 0][0], plus(chip[2, 0][1], over_y(diagonal[1]))]
    out = []
    for own, sent_x, sent_y in zip(chip[0, 0], to_x, to_y):
        out.append(
            (own.astype(F32) + over_x(sent_x).astype(F32) + over_y(sent_y).astype(F32)).astype(BF)
        )
    return jnp.concatenate(out, axis=0)


def sum_over_dp(part):
    if lax.axis_size("dp") != 4:
        return lax.psum(part, "dp").astype(F32)
    place = lax.axis_index("dp")
    inner = (place == 1) | (place == 2)
    came = lax.ppermute(part, "dp", [(0, 1), (3, 2)])
    part = (part.astype(F32) + came.astype(F32)).astype(BF)
    came = lax.ppermute(part, "dp", [(1, 2), (2, 1)])
    part = (part.astype(F32) + came.astype(F32)).astype(BF)
    came = lax.ppermute(part, "dp", [(1, 0), (2, 3)])
    return jnp.where(inner, part, came).astype(F32)


def sum_small(vector):
    size = lax.axis_size("dp")
    for mask in (1, 2):
        vector = vector + swap(vector, "row", mask)
    if size & (size - 1):
        return lax.psum(vector, "dp")
    mask = 1
    while mask < size:
        vector = vector + swap(vector, "dp", mask)
        mask *= 2
    return vector


def norm_forward(values, norm_gain, norm_shift):
    width = values.shape[1]
    mean_val = jnp.sum(values, axis=1, keepdims=True) / width
    var_val = jnp.sum(values * values, axis=1, keepdims=True) / width - mean_val * mean_val
    inv_dev = lax.rsqrt(var_val + EPSILON)
    normed = (values - mean_val) * inv_dev
    return ((normed * norm_gain + norm_shift).astype(BF), normed, inv_dev)


def norm_back(grad_out, normed, inv_dev, norm_gain):
    width = grad_out.shape[1]
    scaled = grad_out * norm_gain
    first_mean = jnp.sum(scaled, axis=1, keepdims=True) / width
    second_mean = jnp.sum(scaled * normed, axis=1, keepdims=True) / width
    return inv_dev * (scaled - first_mean - normed * second_mean)


def attend(query, keys, values):
    scores = jnp.einsum("shd,thd->hst", query, keys, preferred_element_type=F32) * HD ** (-0.5)
    row_top = jnp.max(scores, axis=-1, keepdims=True)
    logsum = row_top + jnp.log(jnp.sum(jnp.exp(scores - row_top), axis=-1, keepdims=True))
    probs = jnp.exp(scores - logsum).astype(BF)
    return jnp.einsum("hst,thd->shd", probs, values, preferred_element_type=F32).astype(BF), logsum


def attend_back(query, keys, values, logsum, grad_out):
    scale = HD ** (-0.5)
    scores = jnp.einsum("shd,thd->hst", query, keys, preferred_element_type=F32) * scale
    soft = jnp.exp(scores - logsum)
    grad_value = jnp.einsum("hst,shd->thd", soft.astype(BF), grad_out, preferred_element_type=F32)
    grad_soft = jnp.einsum("shd,thd->hst", grad_out, values, preferred_element_type=F32)
    row_delta = jnp.sum(soft * grad_soft, axis=-1, keepdims=True)
    grad_scores = (soft * (grad_soft - row_delta)).astype(BF)
    grad_query = jnp.einsum("hst,thd->shd", grad_scores, keys, preferred_element_type=F32) * scale
    grad_key = jnp.einsum("hst,shd->thd", grad_scores, query, preferred_element_type=F32) * scale
    return grad_query.astype(BF), grad_key.astype(BF), grad_value.astype(BF)


def body(
    block_input,
    qkv_weight,
    query_bias,
    value_bias,
    out_weight,
    out_bias,
    first_gain,
    first_shift,
    second_gain,
    second_shift,
    up_weight,
    up_bias,
    down_weight,
    down_bias,
    out_cotangent,
):
    images_all = lax.axis_size("dp") * lax.axis_size("row") * lax.axis_size("col")
    width = qkv_weight.shape[1]
    head_cols = qkv_weight.shape[2]
    heads = head_cols // HD
    hidden_cols = up_weight.shape[1]
    col = lax.axis_index("col")

    def own_image(rows):
        kept = lax.dynamic_slice_in_dim(rows, col * S, S, 0)
        sent = lax.dynamic_slice_in_dim(rows, (1 - col) * S, S, 0)
        return kept, over_y(sent.astype(BF))

    x_own, x_far = own_image(block_input)
    image_in = jnp.concatenate([x_own, x_far.astype(F32)], axis=1)

    column_params = jnp.stack([first_gain, first_shift, second_gain, second_shift, out_bias, down_bias])
    column_params = jnp.concatenate([column_params, over_y(column_params)], axis=1)
    gain1, shift1, gain2, shift2, bias_out, bias_down = [column_params[i] for i in range(6)]
    row_params = jnp.concatenate([up_bias, query_bias, value_bias])[None]
    row_params = [row_params[0]] + [swap(row_params, "row", k)[0] for k in (1, 2, 3)]

    flat_qkv = jnp.transpose(qkv_weight, (1, 0, 2)).reshape(width, 3 * head_cols)
    qkv_all = stack_pieces(gather_weight(flat_qkv))
    out_pieces = gather_weight(out_weight)
    out_all = [
        jnp.concatenate([jnp.concatenate(out_pieces[k, m], axis=0) for m in (0, 1)], axis=1)
        for k in range(4)
    ]
    up_all = stack_pieces(gather_weight(up_weight))
    down_all = stack_pieces(gather_weight(down_weight.T))

    cot_own, cot_far = own_image(out_cotangent)
    cotangent = jnp.concatenate([cot_own, cot_far.astype(F32)], axis=1)
    cot_rounded = cotangent.astype(BF)

    first_normed, first_hat, first_inv = norm_forward(image_in, gain1, shift1)
    saved = []
    attn_sum = 0.0
    for k in range(4):
        projected = dot(first_normed, qkv_all[k], ((1,), (0,)))
        q_bias = row_params[k][hidden_cols : hidden_cols + head_cols]
        v_bias = row_params[k][hidden_cols + head_cols :]
        query = (projected[:, :head_cols] + q_bias).astype(BF).reshape(S, heads, HD)
        keys = projected[:, head_cols : 2 * head_cols].astype(BF).reshape(S, heads, HD)
        values = (projected[:, 2 * head_cols :] + v_bias).astype(BF).reshape(S, heads, HD)
        attended, logsum = attend(query, keys, values)
        attended = attended.reshape(S, head_cols)
        saved.append((query, keys, values, logsum, attended))
        attn_sum = attn_sum + dot(attended, out_all[k], ((1,), (0,)))
    middle = image_in + attn_sum + bias_out
    second_normed, second_hat, second_inv = norm_forward(middle, gain2, shift2)

    mlp_sum = 0.0
    grad_second = 0.0
    up_grads, down_grads = {}, {}
    up_bias_sums = []
    for k in range(4):
        pre_act = dot(second_normed, up_all[k], ((1,), (0,))) + row_params[k][:hidden_cols]
        hidden = gelu_tanh(pre_act).astype(BF)
        grad_hidden = dot(cot_rounded, down_all[k], ((1,), (0,)))
        grad_pre = jax.vjp(gelu_tanh, pre_act)[1](grad_hidden)[0].astype(BF)
        down_grad = dot(cot_rounded, hidden, ((0,), (0,))) / images_all
        up_grad = dot(second_normed, grad_pre, ((0,), (0,))) / images_all
        up_bias_sums.append(jnp.sum(grad_pre, axis=0, dtype=F32) / images_all)
        for m in (0, 1):
            down_grads[k, m] = down_grad[m * width : (m + 1) * width]
            up_grads[k, m] = up_grad[m * width : (m + 1) * width]
        mlp_sum = mlp_sum + dot(hidden, down_all[k], ((1,), (1,)))
        grad_second = grad_second + dot(grad_pre, up_all[k], ((1,), (1,)))
    down_w_grad = sum_over_dp(scatter_grad(down_grads)).T
    up_w_grad = sum_over_dp(scatter_grad(up_grads))
    output = middle + mlp_sum + bias_down

    def column_sums(*arrays):
        return [jnp.sum(array, axis=0, dtype=F32) / images_all for array in arrays]

    grad_middle = cotangent + norm_back(grad_second, second_hat, second_inv, gain2)
    middle_rounded = grad_middle.astype(BF)
    gain2_sum, shift2_sum, out_b_sum, down_b_sum = column_sums(
        grad_second * second_hat, grad_second, middle_rounded, cot_rounded
    )

    out_grads, qkv_grads = {}, {}
    query_sums, value_sums = [], []
    grad_first = 0.0
    for k in range(4):
        query, keys, values, logsum, attended = saved[k]
        out_grad = dot(attended, middle_rounded, ((0,), (0,))) / images_all
        for m in (0, 1):
            out_grads[k, m] = out_grad[:, m * width : (m + 1) * width]
        grad_attended = dot(middle_rounded, out_all[k], ((1,), (1,))).astype(BF)
        grads = attend_back(query, keys, values, logsum, grad_attended.reshape(S, heads, HD))
        grads = [grad.reshape(S, head_cols) for grad in grads]
        query_sums += column_sums(grads[0])
        value_sums += column_sums(grads[2])
        stacked = jnp.concatenate(grads, axis=1)
        qkv_grad = dot(first_normed, stacked, ((0,), (0,))) / images_all
        for m in (0, 1):
            qkv_grads[k, m] = qkv_grad[m * width : (m + 1) * width]
        grad_first = grad_first + dot(stacked, qkv_all[k], ((1,), (1,)))
    out_w_grad = sum_over_dp(scatter_grad(out_grads))
    qkv_w_grad = sum_over_dp(scatter_grad(qkv_grads))
    qkv_w_grad = qkv_w_grad.reshape(width, 3, head_cols).transpose(1, 0, 2)
    gain1_sum, shift1_sum = column_sums(grad_first * first_hat, grad_first)
    grad_input = grad_middle + norm_back(grad_first, first_hat, first_inv, gain1)

    def to_rows(array):
        own, far = array[:, :width], over_y(array[:, width:].astype(BF)).astype(F32)
        both = jnp.zeros((2 * S, width), F32)
        both = lax.dynamic_update_slice_in_dim(both, own, col * S, 0)
        return lax.dynamic_update_slice_in_dim(both, far, (1 - col) * S, 0)

    columns = jnp.stack([gain1_sum, shift1_sum, gain2_sum, shift2_sum, out_b_sum, down_b_sum])
    columns = sum_small(columns[:, :width] + over_y(columns[:, width:]))
    rows = [jnp.concatenate([up_bias_sums[k], query_sums[k], value_sums[k]])[None] for k in range(4)]
    rows_own = rows[0] + sum(swap(rows[k], "row", k) for k in (1, 2, 3))
    rows_own = rows_own + over_y(rows_own)
    mask, size = 1, lax.axis_size("dp")
    while mask < size:
        rows_own = rows_own + swap(rows_own, "dp", mask)
        mask *= 2
    rows_own = rows_own[0]
    return (
        to_rows(output),
        to_rows(grad_input),
        qkv_w_grad,
        rows_own[hidden_cols : hidden_cols + head_cols],
        rows_own[hidden_cols + head_cols :],
        out_w_grad,
        columns[4],
        columns[0],
        columns[1],
        columns[2],
        columns[3],
        up_w_grad,
        rows_own[:hidden_cols],
        down_w_grad,
        columns[5],
    )


def solution(mesh):
    col, row = P("col"), P("row")
    tokens = P(("dp", "row"), "col")
    qkv, out, up = P(None, "col", "row"), P("row", "col"), P("col", "row")
    return jax.shard_map(
        body,
        mesh=mesh,
        in_specs=(tokens, qkv, row, row, out, col, col, col, col, col, up, row, out, col, tokens),
        out_specs=(tokens, tokens, qkv, row, row, out, col, col, col, col, col, up, row, out, col),
        check_vma=False,
    )
```
